32 devices in a mesh: band: 16 (over z, x, core), dom: 2 (over y).
Axes of the slice: x: 2, y: 2, z: 4, core: 2. Of those that a mesh axis runs over, the one named last changes fastest.
Arguments:
- orbitals: bfloat16 [128, 64, 32, 128], P('band', None, 'dom'), may hold values from -6 to 6
- occupations: float32 [128], P('band'), may hold values from 0.25 to 2
Outputs:
- potential: float32 [128, 64, 256], P('band', 'dom')
The draws below stay inside these ranges and needn't reach their ends.
All inputs are finite; a program needn't handle non-finite values.
Results may differ from the reference program's by a relative error of at most 0.0003.
Values sent between devices are 32-bit elements; how exact they have to be, the bound alone decides.
No kernel may reach another device: no remote copies, remote signals or barrier semaphores. Data moves between devices by JAX's collectives and lax.ppermute only.
A program may use at most 64 MiB of HBM per device.

```python
import math
import jax
import jax.numpy as jnp
from jax import lax

N3 = 128
BANDS = 128
N1 = 64
N2 = 32


def raised(result, rng, source, target, shards_of, factor):
    def block_of(dim):
        return (jnp.arange(result.shape[dim]) // (result.shape[dim] // shards_of)).reshape((-1,) + (1,) * (result.ndim - 1 - dim))

    near = jax.random.permutation(rng, shards_of)[block_of(target)]
    second = (block_of(target) + shards_of // 2) % shards_of
    return jnp.where((block_of(source) == near) | (block_of(source) == second), factor * result, result)


def steps_of(stream_key, shape, pieces, low, top_value):
    level, own = 1.0, jax.random.fold_in(stream_key, 6)
    for axis_at, shards_of in pieces:
        draws = jnp.exp(jax.random.uniform(jax.random.fold_in(own, axis_at), (shards_of,), jnp.float32, low / len(pieces), top_value / len(pieces)))
        level = level * jnp.repeat(draws, shape[axis_at] // shards_of).reshape([-1 if axis == axis_at else 1 for axis in range(len(shape))])
    return level


def heavy_noise(rng, dims, scale, reach, shards, heavy, kind=jnp.bfloat16):
    values = scale * jax.random.normal(rng, dims, jnp.float32)
    if shards:
        values = values * steps_of(rng, dims, shards, -0.22, 0.18)
    return jnp.clip(raised(values, jax.random.fold_in(rng, 3), *heavy), -reach, reach).astype(kind)


def setup_inputs(seed: int = 0) -> dict:
    splits = jax.random.split(jax.random.key(seed), 3)
    orbitals = heavy_noise(splits[0], (BANDS, N1, N2, N3), 1.0, 6.0, ((0, 16), (2, 2)), (0, 1, 16, 2.0))
    occupations = jnp.clip(jnp.exp(math.log(2.0) - 2.0794415 * jax.random.uniform(splits[1], (BANDS,), jnp.float32) ** steps_of(splits[1], (BANDS,), ((0, 16),), -0.2, 0.2)), 0.25, 2.0)
    return dict(orbitals=orbitals, occupations=occupations)


interp_weights = (3.0 / 256.0, -25.0 / 256.0, 150.0 / 256.0, 150.0 / 256.0, -25.0 / 256.0, 3.0 / 256.0)
deriv_factors = (4.0 / 5.0, -1.0 / 5.0, 4.0 / 105.0, -1.0 / 280.0)


def alternate(even_cells, odd_cells, along):
    stacked = jnp.stack([even_cells, odd_cells], axis=along + 1)
    target_shape = list(even_cells.shape)
    target_shape[along] = 2 * even_cells.shape[along]
    return stacked.reshape(target_shape)


def refine(padded, along, extent):
    odd_cells = jnp.zeros_like(lax.slice_in_dim(padded, 3, 3 + extent, axis=along))
    for offset, factor in zip(range(-2, 4), interp_weights):
        odd_cells = odd_cells + factor * lax.slice_in_dim(padded, 3 + offset, 3 + offset + extent, axis=along)
    even_cells = lax.slice_in_dim(padded, 3, 3 + extent, axis=along)
    return alternate(even_cells, odd_cells, along)


def central(padded, along, start_a, start_b, extent_a, extent_b):
    window_base = padded[start_a:start_a + extent_a, start_b:start_b + extent_b]
    summed = jnp.zeros_like(window_base)
    for offset, factor in zip((1, 2, 3, 4), deriv_factors):
        if along == 0:
            ahead_part = padded[start_a + offset:start_a + offset + extent_a, start_b:start_b + extent_b]
            behind_part = padded[start_a - offset:start_a - offset + extent_a, start_b:start_b + extent_b]
        elif along == 1:
            ahead_part = padded[start_a:start_a + extent_a, start_b + offset:start_b + offset + extent_b]
            behind_part = padded[start_a:start_a + extent_a, start_b - offset:start_b - offset + extent_b]
        else:
            ahead_part = jnp.roll(window_base, -offset, 2)
            behind_part = jnp.roll(window_base, offset, 2)
        summed = summed + factor * (ahead_part - behind_part)
    return summed


def pointwise(density, grad_a, grad_b, grad_c):
    shifted = density * density + 0.01
    scaling = 0.01 * shifted ** (4.0 / 3.0)
    reduced = (grad_a * grad_a + grad_b * grad_b + grad_c * grad_c) / scaling
    divisor = 1.0 + 0.2195 * reduced / 0.804
    enhance = 0.804 - 0.804 / divisor
    flux_weight = 0.2195 / (divisor * divisor) / scaling
    local_part = -0.75 * shifted ** (1.0 / 6.0) * (1.0 + enhance)
    return local_part, flux_weight * grad_a, flux_weight * grad_b, flux_weight * grad_c


def reference(orbitals, occupations):
    weights = occupations / orbitals.shape[0]

    def add_band(index, summed):
        return summed + weights[index] * jnp.square(orbitals[index].astype(jnp.float32))

    density = lax.fori_loop(0, orbitals.shape[0], add_band, jnp.zeros(orbitals.shape[1:], jnp.float32))
    fine = density
    for along in (0, 1, 2):
        widths = [(0, 0), (0, 0), (0, 0)]
        widths[along] = (3, 3)
        fine = refine(jnp.pad(fine, widths, mode="wrap"), along, fine.shape[along])
    extent_a, extent_b = fine.shape[0], fine.shape[1]
    padded = jnp.pad(fine, ((4, 4), (4, 4), (0, 0)), mode="wrap")
    grad_a = central(padded, 0, 4, 4, extent_a, extent_b)
    grad_b = central(padded, 1, 4, 4, extent_a, extent_b)
    grad_c = central(padded, 2, 4, 4, extent_a, extent_b)
    local_part, flux_a, flux_b, flux_c = pointwise(fine, grad_a, grad_b, grad_c)
    div_a = central(jnp.pad(flux_a, ((4, 4), (0, 0), (0, 0)), mode="wrap"), 0, 4, 0, extent_a, extent_b)
    div_b = central(jnp.pad(flux_b, ((0, 0), (4, 4), (0, 0)), mode="wrap"), 1, 0, 4, extent_a, extent_b)
    div_c = central(flux_c, 2, 0, 0, extent_a, extent_b)
    return local_part + 0.2 * (div_a + div_b + div_c)
```

```python
import functools

import jax
import jax.numpy as jnp
import numpy as np
from jax import lax
from jax.experimental import pallas as pl
from jax.experimental.pallas import tpu as pltpu
from jax.sharding import PartitionSpec as P

interp_weights = (
    3.0 / 256.0,
    -25.0 / 256.0,
    150.0 / 256.0,
    150.0 / 256.0,
    -25.0 / 256.0,
    3.0 / 256.0,
)
deriv_factors = (4.0 / 5.0, -1.0 / 5.0, 4.0 / 105.0, -1.0 / 280.0)
BEFORE, AFTER = 6, 7
SIDE = 8
HIGHEST = lax.Precision.HIGHEST


def third_matrices(cells):
    refine = np.zeros((cells, 2 * cells))
    for i in range(cells):
        refine[i, 2 * i] = 1.0
        for offset, factor in zip(range(-2, 4), interp_weights):
            refine[(i + offset) % cells, 2 * i + 1] += factor
    derive = np.zeros((2 * cells, 2 * cells))
    for i in range(2 * cells):
        for offset, factor in zip((1, 2, 3, 4), deriv_factors):
            derive[(i + offset) % (2 * cells), i] += factor
            derive[(i - offset) % (2 * cells), i] -= factor
    return (
        np.concatenate([refine, refine @ derive], axis=1).astype(np.float32),
        derive.astype(np.float32),
    )


def density_kernel(scale, which_ref, occupations_ref, orbitals_ref, out_ref):
    total = None
    for band in range(orbitals_ref.shape[0]):
        value = orbitals_ref[band, :, 0].astype(jnp.float32)
        term = (occupations_ref[band] * scale) * (value * value)
        total = term if total is None else total + term
    out_ref[...] = total


def partial_density(orbitals, occupations, which, scale):
    bands, blocks, _, rows, columns, lanes = orbitals.shape
    group = 2 if blocks % 2 == 0 else 1
    return pl.pallas_call(
        functools.partial(density_kernel, scale),
        out_shape=jax.ShapeDtypeStruct((blocks, rows, columns, lanes), jnp.float32),
        grid_spec=pltpu.PrefetchScalarGridSpec(
            num_scalar_prefetch=1,
            grid=(blocks // group,),
            in_specs=[
                pl.BlockSpec(memory_space=pltpu.SMEM),
                pl.BlockSpec(
                    (bands, group, 1, rows, columns, lanes),
                    lambda g, which_ref: (0, g, which_ref[0], 0, 0, 0),
                ),
            ],
            out_specs=pl.BlockSpec((group, rows, columns, lanes), lambda g, which_ref: (g, 0, 0, 0)),
        ),
        cost_estimate=pl.CostEstimate(
            flops=4 * bands * blocks * rows * columns * lanes,
            bytes_accessed=(2 * bands + 4) * blocks * rows * columns * lanes,
            transcendentals=0,
        ),
    )(which, occupations, orbitals)


def difference(load):
    total = None
    for offset, factor in zip((1, 2, 3, 4), deriv_factors):
        term = factor * (load(offset) - load(-offset))
        total = term if total is None else total + term
    return total


def stencil(load):
    a = load(0) + load(1)
    b = load(-1) + load(2)
    c = load(-2) + load(3)
    return interp_weights[2] * a + interp_weights[1] * b + interp_weights[0] * c


def tail_kernel(counts, *refs):
    pieces = refs[: len(counts)]
    refine_ref, derive_ref, out_ref, rows_ref, mixed_ref, fine_ref, grad_ref, flux_ref, side_ref, third_ref, local_ref = refs[len(counts) :]
    layers = [(piece, row) for piece, count in zip(pieces, counts) for row in range(count)]
    extent_a, extent_b, _ = out_ref.shape
    lanes = pieces[0].shape[2]
    wide_a, wide_b = extent_a + 16, extent_b + 16
    half_b = wide_b // 2

    def coarse(index):
        piece, row = layers[index]
        return piece[row]

    for index in range(wide_a):
        at = index // 2 + 2
        if index % 2 == 0:
            rows_ref[index] = coarse(at)
        else:
            rows_ref[index] = stencil(lambda offset: coarse(at + offset))
        first = SIDE - 4
        mixed_ref[index, pl.ds(0, half_b, stride=2), :] = rows_ref[index, first : first + half_b, :]
        mixed_ref[index, pl.ds(1, half_b, stride=2), :] = stencil(
            lambda offset: rows_ref[index, first + offset : first + offset + half_b, :]
        )
    for index in range(wide_a):
        inner = 4 <= index < wide_a - 4
        matrix = refine_ref[...] if inner else refine_ref[:, : 2 * lanes]
        product = jnp.dot(mixed_ref[index], matrix, preferred_element_type=jnp.float32, precision=HIGHEST)
        for half in range(2):
            fine_ref[half, index] = product[:, half * lanes : (half + 1) * lanes]
            if inner:
                grad_ref[half, index - 4] = product[:, (2 + half) * lanes : (3 + half) * lanes]
    for index in range(extent_a + 8):
        own = 4 <= index < extent_a + 4
        low, high = (4, wide_b - 4) if own else (8, wide_b - 8)
        for half in range(2):
            at = index + 4
            density = fine_ref[half, at, low:high, :]
            grad_a = difference(lambda offset: fine_ref[half, at + offset, low:high, :])
            grad_b = difference(lambda offset: fine_ref[half, at, low + offset : high + offset, :])
            grad_c = grad_ref[half, index, low:high, :]
            shifted = density * density + 0.01
            root = jnp.exp(jnp.log(shifted) * (1.0 / 6.0))
            scaling = 0.01 * (shifted * (root * root))
            square = grad_a * grad_a + grad_b * grad_b + grad_c * grad_c
            inverse = 1.0 / (scaling + (0.2195 / 0.804) * square)
            ratio = scaling * inverse
            weight = 0.2195 * (ratio * inverse)
            flux_ref[half, index, low:high, :] = weight * grad_a
            if own:
                side_ref[half, index - 4, low:high, :] = weight * grad_b
                third_ref[half, index - 4, low:high, :] = weight * grad_c
                local_ref[half, index - 4, low:high, :] = -0.75 * root * (1.804 - 0.804 * ratio)
    for index in range(extent_a):
        third = jnp.concatenate([third_ref[half, index, 8 : 8 + extent_b, :] for half in range(2)], axis=1)
        third = jnp.dot(third, derive_ref[...], preferred_element_type=jnp.float32, precision=HIGHEST)
        for half in range(2):
            part = slice(half * lanes, (half + 1) * lanes)
            total = difference(lambda offset: flux_ref[half, index + 4 + offset, 8 : 8 + extent_b, :])
            total = total + difference(lambda offset: side_ref[half, index, 8 + offset : 8 + offset + extent_b, :])
            out_ref[index, :, part] = local_ref[half, index, 8 : 8 + extent_b, :] + 0.2 * (total + third[:, part])


def tail(pieces, counts, rows, columns):
    lanes = pieces[0].shape[2]
    extent_a, extent_b = 2 * rows, 2 * columns
    wide_a, wide_b = extent_a + 16, extent_b + 16
    refine, derive = third_matrices(lanes)
    points = wide_a * wide_b * 2 * lanes
    scratch = lambda *shape: pltpu.VMEM(shape, jnp.float32)
    return pl.pallas_call(
        functools.partial(tail_kernel, counts),
        out_shape=jax.ShapeDtypeStruct((extent_a, extent_b, 2 * lanes), jnp.float32),
        in_specs=[pl.BlockSpec(memory_space=pltpu.VMEM)] * (len(pieces) + 2),
        out_specs=pl.BlockSpec(memory_space=pltpu.VMEM),
        scratch_shapes=[
            scratch(wide_a, columns + 2 * SIDE, lanes),
            scratch(wide_a, wide_b, lanes),
            scratch(2, wide_a, wide_b, lanes),
            scratch(2, extent_a + 8, wide_b, lanes),
            scratch(2, extent_a + 8, wide_b, lanes),
            scratch(2, extent_a, wide_b, lanes),
            scratch(2, extent_a, wide_b, lanes),
            scratch(2, extent_a, wide_b, lanes),
        ],
        cost_estimate=pl.CostEstimate(
            flops=100 * points, bytes_accessed=8 * points, transcendentals=2 * points
        ),
    )(*pieces, jnp.asarray(refine), jnp.asarray(derive))


def shift(value, axis, step):
    devices = lax.axis_size(axis)
    return lax.ppermute(value, axis, [(i, (i + step) % devices) for i in range(devices)])


def with_sides(block):
    columns, devices = block.shape[1], lax.axis_size("dom")
    last, first = block[:, columns - SIDE :], block[:, :SIDE]
    if devices == 1:
        before, after = last, first
    elif devices == 2:
        other = shift(block, "dom", 1)
        before, after = other[:, columns - SIDE :], other[:, :SIDE]
    else:
        before, after = shift(last, "dom", 1), shift(first, "dom", -1)
    return jnp.concatenate([before, block, after], axis=1)


def with_layers(block):
    rows = block.shape[0]
    before, after = [], []
    step, missing = 1, BEFORE
    while missing > 0:
        count = min(rows, missing)
        before.insert(0, shift(block[rows - count :], "band", step))
        step, missing = step + 1, missing - count
    step, missing = 1, AFTER
    while missing > 0:
        count = min(rows, missing)
        after.append(shift(block[:count], "band", -step))
        step, missing = step + 1, missing - count
    return before + [block] + after


def on_device(orbitals, occupations):
    devices = lax.axis_size("band")
    bands, layers, columns, lanes = orbitals.shape
    rows = layers // devices
    place = lax.axis_index("band")
    scale = 1.0 / (bands * devices)
    blocks = orbitals.reshape(bands, devices // 2, 2, rows, columns, lanes)
    parity = lax.rem(place, 2)
    send = partial_density(blocks, occupations, jnp.reshape(1 - parity, (1,)).astype(jnp.int32), scale)
    keep = partial_density(blocks, occupations, jnp.reshape(parity, (1,)).astype(jnp.int32), scale)
    width = 1
    while True:
        density = keep + lax.ppermute(send, "band", [(i, i ^ width) for i in range(devices)])
        width = 2 * width
        if width == devices:
            break
        bit = lax.rem(lax.div(place, width), 2)
        pairs = density.reshape((devices // width // 2, 2, rows, columns, lanes))
        keep = lax.dynamic_index_in_dim(pairs, bit, 1, False)
        send = lax.dynamic_index_in_dim(pairs, 1 - bit, 1, False)
    block = with_sides(density[0])
    pieces = with_layers(block)
    return tail(pieces, tuple(piece.shape[0] for piece in pieces), rows, columns)


def solution(mesh):
    return jax.shard_map(
        on_device,
        mesh=mesh,
        in_specs=(P("band", None, "dom", None), P("band")),
        out_specs=P("band", "dom", None),
        check_vma=False,
    )
```

```python
import functools

import jax
import jax.numpy as jnp
import ml_dtypes
import numpy as np
from jax import lax
from jax.experimental import pallas as pl
from jax.experimental.pallas import tpu as pltpu
from jax.sharding import PartitionSpec as P

interp_weights = (
    3.0 / 256.0,
    -25.0 / 256.0,
    150.0 / 256.0,
    150.0 / 256.0,
    -25.0 / 256.0,
    3.0 / 256.0,
)
deriv_factors = (4.0 / 5.0, -1.0 / 5.0, 4.0 / 105.0, -1.0 / 280.0)
BEFORE, AFTER = 6, 7
VMEM_LIMIT = 16 * 1024 * 1024
bf16 = ml_dtypes.bfloat16


def split_matrix(matrix):
    high = matrix.astype(bf16)
    return high, (matrix - high.astype(np.float64)).astype(bf16)


def third_matrices(cells):
    refine = np.zeros((cells, 2 * cells))
    for i in range(cells):
        refine[i, 2 * i] = 1.0
        for offset, factor in zip(range(-2, 4), interp_weights):
            refine[(i + offset) % cells, 2 * i + 1] += factor
    derive = np.zeros((2 * cells, 2 * cells))
    for i in range(2 * cells):
        for offset, factor in zip((1, 2, 3, 4), deriv_factors):
            derive[(i + offset) % (2 * cells), i] += factor
            derive[(i - offset) % (2 * cells), i] -= factor
    twice = lambda matrix: np.concatenate([matrix, matrix], axis=0)
    both = split_matrix(twice(refine @ derive))
    return np.concatenate([twice(refine).astype(bf16), *both, *split_matrix(derive)], axis=1)


def density_kernel(scale, other, occupations_ref, orbitals_ref, out_ref, buffer_ref, sems):
    bands, layers, half, _ = buffer_ref.shape
    core = lax.rem(lax.axis_index("band"), 2)
    start = pl.multiple_of((1 - core if other else core) * half, half)
    chunk = layers // sems.shape[0]
    copies = []
    for index in range(sems.shape[0]):
        rows = pl.ds(index * chunk, chunk)
        copy = pltpu.make_async_copy(
            orbitals_ref.at[:, rows, pl.ds(start, half), :], buffer_ref.at[:, rows], sems.at[index]
        )
        copy.start()
        copies.append(copy)
    for index, copy in enumerate(copies):
        copy.wait()
        rows = slice(index * chunk, (index + 1) * chunk)
        total = None
        for band in range(bands):
            value = buffer_ref[band, rows].astype(jnp.float32)
            term = (occupations_ref[band] * scale) * (value * value)
            total = term if total is None else total + term
        out_ref[rows] = total


def partial_density(orbitals, occupations, scale, other):
    bands, layers, columns, lanes = orbitals.shape
    half = columns // 2
    points = layers * half * lanes
    return pl.pallas_call(
        functools.partial(density_kernel, scale, other),
        out_shape=jax.ShapeDtypeStruct((layers, half, lanes), jnp.float32),
        in_specs=[pl.BlockSpec(memory_space=pltpu.SMEM), pl.BlockSpec(memory_space=pl.ANY)],
        out_specs=pl.BlockSpec(memory_space=pltpu.VMEM),
        scratch_shapes=[pltpu.VMEM((bands, layers, half, lanes), orbitals.dtype), pltpu.SemaphoreType.DMA((4,))],
        compiler_params=pltpu.CompilerParams(vmem_limit_bytes=VMEM_LIMIT),
        cost_estimate=pl.CostEstimate(
            flops=4 * bands * points, bytes_accessed=(2 * bands + 4) * points, transcendentals=0
        ),
    )(occupations, orbitals)


def combine_kernel(planes, keep_ref, other_ref, *out_refs):
    layers, count = keep_ref.shape[0], out_refs[0].shape[0]
    plane = lax.div(lax.axis_index("band"), 4)
    for step, out_ref in enumerate(out_refs):
        first = lax.rem(plane + step, planes) * (layers // planes) + (layers - BEFORE)
        for row in range(count):
            at = lax.rem(first + row, layers)
            out_ref[row] = keep_ref[at] + other_ref[at]


def combine(keep, other, planes):
    layers, half, lanes = keep.shape
    shape = jax.ShapeDtypeStruct((layers // planes + BEFORE + AFTER, half, lanes), jnp.float32)
    return pl.pallas_call(
        functools.partial(combine_kernel, planes),
        out_shape=[shape] * planes,
        in_specs=[pl.BlockSpec(memory_space=pltpu.VMEM)] * 2,
        out_specs=[pl.BlockSpec(memory_space=pltpu.VMEM)] * planes,
        compiler_params=pltpu.CompilerParams(vmem_limit_bytes=VMEM_LIMIT),
    )(keep, other)


def difference(load):
    total = None
    for offset, factor in zip((1, 2, 3, 4), deriv_factors):
        term = factor * (load(offset) - load(-offset))
        total = term if total is None else total + term
    return total


def stencil(load):
    a = load(0) + load(1)
    b = load(-1) + load(2)
    c = load(-2) + load(3)
    return interp_weights[2] * a + interp_weights[1] * b + interp_weights[0] * c


def split_value(value):
    high = value.astype(jnp.bfloat16)
    return high, (value - high.astype(jnp.float32)).astype(jnp.bfloat16)


def product(left, right):
    return jnp.dot(left, right, preferred_element_type=jnp.float32)


def tail_kernel(mine_ref, other_ref, matrix_ref, out_ref, coarse_ref, rows_ref, mixed_ref, fine_ref, grad_ref, flux_ref, side_ref, third_ref, local_ref):
    extent_a, extent_b, _ = out_ref.shape
    half, lanes = mine_ref.shape[2:]
    wide_a, wide_b = extent_a + 16, extent_b + 16
    half_b = wide_b // 2
    core = lax.rem(lax.axis_index("band"), 2)
    for tile, (owner, side) in enumerate(((1, 1), (0, 0), (1, 0), (0, 1))):
        coarse_ref[:, tile * half : (tile + 1) * half, :] = jnp.where(
            core == owner, mine_ref[side], other_ref[side]
        )
    first = half - 4
    for index in range(wide_a):
        at = index // 2 + BEFORE - 4
        if index % 2 == 0:
            rows_ref[index] = coarse_ref[at]
        else:
            rows_ref[index] = stencil(lambda offset: coarse_ref[at + offset])
        mixed_ref[index, pl.ds(0, half_b, stride=2), :] = rows_ref[index, first : first + half_b, :]
        mixed_ref[index, pl.ds(1, half_b, stride=2), :] = stencil(
            lambda offset: rows_ref[index, first + offset : first + offset + half_b, :]
        )
    wide = 2 * lanes
    group = 4
    for start in range(0, wide_a, group):
        value = mixed_ref[start : start + group].reshape(group * wide_b, lanes)
        value = jnp.concatenate(split_value(value), axis=1)
        fine = product(value, matrix_ref[:, :wide]).reshape(group, wide_b, wide)
        for part in range(2):
            fine_ref[part, start : start + group] = fine[:, :, part * lanes : (part + 1) * lanes]
        if 4 <= start < wide_a - 4:
            grad = product(value, matrix_ref[:, wide : 2 * wide]) + product(value, matrix_ref[:, 2 * wide : 3 * wide])
            grad = grad.reshape(group, wide_b, wide)
            for part in range(2):
                grad_ref[part, start - 4 : start - 4 + group] = grad[:, :, part * lanes : (part + 1) * lanes]
    for index in range(extent_a + 8):
        own = 4 <= index < extent_a + 4
        low, high = (4, wide_b - 4) if own else (8, wide_b - 8)
        for part in range(2):
            at = index + 4
            density = fine_ref[part, at, low:high, :]
            grad_a = difference(lambda offset: fine_ref[part, at + offset, low:high, :])
            grad_b = difference(lambda offset: fine_ref[part, at, low + offset : high + offset, :])
            grad_c = grad_ref[part, index, low:high, :]
            shifted = density * density + 0.01
            root = jnp.exp(jnp.log(shifted) * (1.0 / 6.0))
            scaling = 0.01 * (shifted * (root * root))
            square = grad_a * grad_a + grad_b * grad_b + grad_c * grad_c
            inverse = 1.0 / (scaling + (0.2195 / 0.804) * square)
            ratio = scaling * inverse
            weight = 0.2195 * (ratio * inverse)
            flux_ref[part, index, low:high, :] = weight * grad_a
            if own:
                side_ref[part, index - 4, low:high, :] = weight * grad_b
                third_ref[part, index - 4, low:high, :] = weight * grad_c
                local_ref[part, index - 4, low:high, :] = -0.75 * root * (1.804 - 0.804 * ratio)
    for index in range(extent_a):
        third = jnp.concatenate([third_ref[part, index, 8 : 8 + extent_b, :] for part in range(2)], axis=1)
        high, low = split_value(third)
        third = product(high, matrix_ref[:, 3 * wide : 4 * wide]) + (
            product(low, matrix_ref[:, 3 * wide : 4 * wide]) + product(high, matrix_ref[:, 4 * wide : 5 * wide])
        )
        for part in range(2):
            at = slice(part * lanes, (part + 1) * lanes)
            total = difference(lambda offset: flux_ref[part, index + 4 + offset, 8 : 8 + extent_b, :])
            total = total + difference(lambda offset: side_ref[part, index, 8 + offset : 8 + offset + extent_b, :])
            out_ref[index, :, at] = local_ref[part, index, 8 : 8 + extent_b, :] + 0.2 * (total + third[:, at])


def tail(mine, other, rows):
    _, window, half, lanes = mine.shape
    extent_a, extent_b = 2 * rows, 4 * half
    wide_a, wide_b = extent_a + 16, extent_b + 16
    points = wide_a * wide_b * 2 * lanes
    scratch = lambda *shape: pltpu.VMEM(shape, jnp.float32)
    return pl.pallas_call(
        tail_kernel,
        out_shape=jax.ShapeDtypeStruct((extent_a, extent_b, 2 * lanes), jnp.float32),
        in_specs=[pl.BlockSpec(memory_space=pltpu.VMEM)] * 3,
        out_specs=pl.BlockSpec(memory_space=pltpu.VMEM),
        scratch_shapes=[
            scratch(window, 4 * half, lanes),
            scratch(wide_a, 4 * half, lanes),
            scratch(wide_a, wide_b, lanes),
            scratch(2, wide_a, wide_b, lanes),
            scratch(2, extent_a + 8, wide_b, lanes),
            scratch(2, extent_a + 8, wide_b, lanes),
            scratch(2, extent_a, wide_b, lanes),
            scratch(2, extent_a, wide_b, lanes),
            scratch(2, extent_a, wide_b, lanes),
        ],
        compiler_params=pltpu.CompilerParams(vmem_limit_bytes=VMEM_LIMIT),
        cost_estimate=pl.CostEstimate(
            flops=100 * points, bytes_accessed=8 * points, transcendentals=2 * points
        ),
    )(mine, other, jnp.asarray(third_matrices(lanes)))


def on_device(orbitals, occupations):
    devices, domains = lax.axis_size("band"), lax.axis_size("dom")
    bands, layers, columns, lanes = orbitals.shape
    rows, half, planes = layers // devices, columns // 2, devices // 4
    place = lax.axis_index("band")
    core, side = lax.rem(place, 2), lax.rem(lax.div(place, 2), 2)
    scale = 1.0 / (bands * devices)
    swap_cores = [(i, i ^ 1) for i in range(devices)]

    send = partial_density(orbitals, occupations, scale, True)
    other = lax.ppermute(send, "band", swap_cores)
    keep = partial_density(orbitals, occupations, scale, False)
    total, *sends = combine(keep, other, planes)
    for step, value in enumerate(sends, 1):
        total = total + lax.ppermute(value, "band", [(i, (i + 4 * step) % devices) for i in range(devices)])

    def to(turn, move):
        pairs = []
        for i in range(devices):
            for j in range(domains):
                there = (j + (1 if i % 2 else -1)) % domains if move else j
                pairs.append((i * domains + j, (i ^ turn) * domains + there))
        return pairs

    both = ("band", "dom")
    window = 2 * rows + BEFORE + AFTER
    mine = lax.dynamic_slice_in_dim(total, 2 * rows * side, window, 0)
    theirs = lax.dynamic_slice_in_dim(total, 2 * rows * (1 - side), window, 0)
    own = mine + lax.ppermute(theirs, both, to(2, False))
    beside = lax.ppermute(mine, both, to(0, True)) + lax.ppermute(theirs, both, to(2, True))
    blocks = jnp.stack([own, beside])
    window = rows + BEFORE + AFTER
    mine = lax.dynamic_slice_in_dim(blocks, rows * core, window, 1)
    theirs = lax.dynamic_slice_in_dim(blocks, rows * (1 - core), window, 1)
    return tail(mine, lax.ppermute(theirs, "band", swap_cores), rows)


def solution(mesh):
    return jax.shard_map(
        on_device,
        mesh=mesh,
        in_specs=(P("band", None, "dom", None), P("band")),
        out_specs=P("band", "dom", None),
        check_vma=False,
    )
```

```python
import functools

import jax
import jax.numpy as jnp
import ml_dtypes
import numpy as np
from jax import lax
from jax.experimental import pallas as pl
from jax.experimental.pallas import tpu as pltpu
from jax.sharding import PartitionSpec as P

interp_weights = (
    3.0 / 256.0,
    -25.0 / 256.0,
    150.0 / 256.0,
    150.0 / 256.0,
    -25.0 / 256.0,
    3.0 / 256.0,
)
deriv_factors = (4.0 / 5.0, -1.0 / 5.0, 4.0 / 105.0, -1.0 / 280.0)
BEFORE, AFTER = 6, 7
VMEM_LIMIT = 16 * 1024 * 1024
bf16 = ml_dtypes.bfloat16


def split_matrix(matrix):
    high = matrix.astype(bf16)
    return high, (matrix - high.astype(np.float64)).astype(bf16)


def third_matrices(cells):
    refine = np.zeros((cells, 2 * cells))
    for i in range(cells):
        refine[i, 2 * i] = 1.0
        for offset, factor in zip(range(-2, 4), interp_weights):
            refine[(i + offset) % cells, 2 * i + 1] += factor
    derive = np.zeros((2 * cells, 2 * cells))
    for i in range(2 * cells):
        for offset, factor in zip((1, 2, 3, 4), deriv_factors):
            derive[(i + offset) % (2 * cells), i] += factor
            derive[(i - offset) % (2 * cells), i] -= factor
    twice = lambda matrix: np.concatenate([matrix, matrix], axis=0)
    both = split_matrix(twice(refine @ derive))
    return np.concatenate([twice(refine).astype(bf16), *both, *split_matrix(derive)], axis=1)


def band_sum(weight, values_ref, rows):
    total = None
    for band in range(values_ref.shape[0]):
        value = values_ref[band, rows].astype(jnp.float32)
        term = weight(band) * (value * value)
        total = term if total is None else total + term
    return total


def send_kernel(scale, occupations_ref, orbitals_ref, out_ref, held_ref, spread_ref, buffer_ref, weights_ref, sems, weights_sem, held_sem):
    bands, layers, half, _ = buffer_ref.shape
    core = lax.rem(lax.axis_index("band"), 2)
    columns = lambda which: pl.ds(pl.multiple_of(which * half, half), half)
    weights_copy = pltpu.make_async_copy(occupations_ref, weights_ref, weights_sem)
    weights_copy.start()
    chunk = layers // sems.shape[0]
    copies = []
    for index in range(sems.shape[0]):
        rows = pl.ds(index * chunk, chunk)
        copy = pltpu.make_async_copy(
            orbitals_ref.at[:, rows, columns(1 - core), :], buffer_ref.at[:, rows], sems.at[index]
        )
        copy.start()
        copies.append(copy)
    held_copy = pltpu.make_async_copy(orbitals_ref.at[:, :, columns(core), :], held_ref, held_sem)
    held_copy.start()
    weights_copy.wait()
    for band in range(bands):
        spread_ref[band] = jnp.full(spread_ref.shape[1:], weights_ref[band] * scale, jnp.float32)
    for index, copy in enumerate(copies):
        copy.wait()
        rows = slice(index * chunk, (index + 1) * chunk)
        out_ref[rows] = band_sum(lambda band: weights_ref[band] * scale, buffer_ref, rows)
    held_copy.wait()


def keep_kernel(held_ref, spread_ref, out_ref):
    layers = out_ref.shape[0]
    for start in range(0, layers, 16):
        rows = slice(start, min(start + 16, layers))
        out_ref[rows] = band_sum(lambda band: spread_ref[band], held_ref, rows)


def partial_densities(orbitals, occupations, scale):
    bands, layers, columns, lanes = orbitals.shape
    half = columns // 2
    points = layers * half * lanes
    density = jax.ShapeDtypeStruct((layers, half, lanes), jnp.float32)
    held = jax.ShapeDtypeStruct((bands, layers, half, lanes), orbitals.dtype)
    spread = jax.ShapeDtypeStruct((bands, half, lanes), jnp.float32)
    in_vmem = pl.BlockSpec(memory_space=pltpu.VMEM)
    in_hbm = lambda value: pltpu.with_memory_space_constraint(value, pltpu.MemorySpace.HBM)
    params = pltpu.CompilerParams(vmem_limit_bytes=VMEM_LIMIT)
    cost = pl.CostEstimate(flops=4 * bands * points, bytes_accessed=4 * bands * points, transcendentals=0)
    send, held, spread = pl.pallas_call(
        functools.partial(send_kernel, scale),
        out_shape=[density, held, spread],
        in_specs=[pl.BlockSpec(memory_space=pltpu.MemorySpace.HBM)] * 2,
        out_specs=[in_vmem] * 3,
        scratch_shapes=[
            pltpu.VMEM(held.shape, held.dtype),
            pltpu.SMEM((bands,), jnp.float32),
            pltpu.SemaphoreType.DMA((4,)),
            pltpu.SemaphoreType.DMA,
            pltpu.SemaphoreType.DMA,
        ],
        compiler_params=params,
        cost_estimate=cost,
    )(in_hbm(occupations), in_hbm(orbitals))
    keep = lambda: pl.pallas_call(
        keep_kernel,
        out_shape=density,
        in_specs=[in_vmem] * 2,
        out_specs=in_vmem,
        compiler_params=params,
        cost_estimate=cost,
    )(held, spread)
    return send, keep


def combine_kernel(planes, keep_ref, other_ref, *out_refs):
    layers, count = keep_ref.shape[0], out_refs[0].shape[0]
    plane = lax.div(lax.axis_index("band"), 4)
    for step, out_ref in enumerate(out_refs):
        first = lax.rem(plane + step, planes) * (layers // planes) + (layers - BEFORE)
        for row in range(count):
            at = lax.rem(first + row, layers)
            out_ref[row] = keep_ref[at] + other_ref[at]


def combine(keep, other, planes):
    layers, half, lanes = keep.shape
    shape = jax.ShapeDtypeStruct((layers // planes + BEFORE + AFTER, half, lanes), jnp.float32)
    return pl.pallas_call(
        functools.partial(combine_kernel, planes),
        out_shape=[shape] * planes,
        in_specs=[pl.BlockSpec(memory_space=pltpu.VMEM)] * 2,
        out_specs=[pl.BlockSpec(memory_space=pltpu.VMEM)] * planes,
        compiler_params=pltpu.CompilerParams(vmem_limit_bytes=VMEM_LIMIT),
    )(keep, other)


def difference(load):
    total = None
    for offset, factor in zip((1, 2, 3, 4), deriv_factors):
        term = factor * (load(offset) - load(-offset))
        total = term if total is None else total + term
    return total


def stencil(load):
    a = load(0) + load(1)
    b = load(-1) + load(2)
    c = load(-2) + load(3)
    return interp_weights[2] * a + interp_weights[1] * b + interp_weights[0] * c


def split_value(value):
    high = value.astype(jnp.bfloat16)
    return high, (value - high.astype(jnp.float32)).astype(jnp.bfloat16)


def product(left, right):
    return jnp.dot(left, right, preferred_element_type=jnp.float32)


def tail_kernel(mine_ref, other_ref, matrix_ref, out_ref, coarse_ref, rows_ref, mixed_ref, fine_ref, grad_ref, flux_ref, side_ref, third_ref, local_ref):
    extent_a, extent_b, _ = out_ref.shape
    half, lanes = mine_ref.shape[2:]
    wide_a, wide_b = extent_a + 16, extent_b + 16
    half_b = wide_b // 2
    core = lax.rem(lax.axis_index("band"), 2)
    for tile, (owner, side) in enumerate(((1, 1), (0, 0), (1, 0), (0, 1))):
        coarse_ref[:, tile * half : (tile + 1) * half, :] = jnp.where(
            core == owner, mine_ref[side], other_ref[side]
        )
    first = half - 4
    for index in range(wide_a):
        at = index // 2 + BEFORE - 4
        if index % 2 == 0:
            rows_ref[index] = coarse_ref[at]
        else:
            rows_ref[index] = stencil(lambda offset: coarse_ref[at + offset])
        mixed_ref[index, pl.ds(0, half_b, stride=2), :] = rows_ref[index, first : first + half_b, :]
        mixed_ref[index, pl.ds(1, half_b, stride=2), :] = stencil(
            lambda offset: rows_ref[index, first + offset : first + offset + half_b, :]
        )
    wide = 2 * lanes
    group = 4
    for start in range(0, wide_a, group):
        value = mixed_ref[start : start + group].reshape(group * wide_b, lanes)
        value = jnp.concatenate(split_value(value), axis=1)
        fine = product(value, matrix_ref[:, :wide]).reshape(group, wide_b, wide)
        for part in range(2):
            fine_ref[part, start : start + group] = fine[:, :, part * lanes : (part + 1) * lanes]
        if 4 <= start < wide_a - 4:
            grad = product(value, matrix_ref[:, wide : 2 * wide]) + product(value, matrix_ref[:, 2 * wide : 3 * wide])
            grad = grad.reshape(group, wide_b, wide)
            for part in range(2):
                grad_ref[part, start - 4 : start - 4 + group] = grad[:, :, part * lanes : (part + 1) * lanes]
    for index in range(extent_a + 8):
        own = 4 <= index < extent_a + 4
        low, high = (4, wide_b - 4) if own else (8, wide_b - 8)
        for part in range(2):
            at = index + 4
            density = fine_ref[part, at, low:high, :]
            grad_a = difference(lambda offset: fine_ref[part, at + offset, low:high, :])
            grad_b = difference(lambda offset: fine_ref[part, at, low + offset : high + offset, :])
            grad_c = grad_ref[part, index, low:high, :]
            shifted = density * density + 0.01
            root = jnp.exp(jnp.log(shifted) * (1.0 / 6.0))
            scaling = 0.01 * (shifted * (root * root))
            square = grad_a * grad_a + grad_b * grad_b + grad_c * grad_c
            inverse = 1.0 / (scaling + (0.2195 / 0.804) * square)
            ratio = scaling * inverse
            weight = 0.2195 * (ratio * inverse)
            flux_ref[part, index, low:high, :] = weight * grad_a
            if own:
                side_ref[part, index - 4, low:high, :] = weight * grad_b
                third_ref[part, index - 4, low:high, :] = weight * grad_c
                local_ref[part, index - 4, low:high, :] = -0.75 * root * (1.804 - 0.804 * ratio)
    for index in range(extent_a):
        third = jnp.concatenate([third_ref[part, index, 8 : 8 + extent_b, :] for part in range(2)], axis=1)
        high, low = split_value(third)
        third = product(high, matrix_ref[:, 3 * wide : 4 * wide]) + (
            product(low, matrix_ref[:, 3 * wide : 4 * wide]) + product(high, matrix_ref[:, 4 * wide : 5 * wide])
        )
        for part in range(2):
            at = slice(part * lanes, (part + 1) * lanes)
            total = difference(lambda offset: flux_ref[part, index + 4 + offset, 8 : 8 + extent_b, :])
            total = total + difference(lambda offset: side_ref[part, index, 8 + offset : 8 + offset + extent_b, :])
            out_ref[index, :, at] = local_ref[part, index, 8 : 8 + extent_b, :] + 0.2 * (total + third[:, at])


def tail(mine, other, rows):
    _, window, half, lanes = mine.shape
    extent_a, extent_b = 2 * rows, 4 * half
    wide_a, wide_b = extent_a + 16, extent_b + 16
    points = wide_a * wide_b * 2 * lanes
    scratch = lambda *shape: pltpu.VMEM(shape, jnp.float32)
    return pl.pallas_call(
        tail_kernel,
        out_shape=jax.ShapeDtypeStruct((extent_a, extent_b, 2 * lanes), jnp.float32),
        in_specs=[pl.BlockSpec(memory_space=pltpu.VMEM)] * 3,
        out_specs=pl.BlockSpec(memory_space=pltpu.VMEM),
        scratch_shapes=[
            scratch(window, 4 * half, lanes),
            scratch(wide_a, 4 * half, lanes),
            scratch(wide_a, wide_b, lanes),
            scratch(2, wide_a, wide_b, lanes),
            scratch(2, extent_a + 8, wide_b, lanes),
            scratch(2, extent_a + 8, wide_b, lanes),
            scratch(2, extent_a, wide_b, lanes),
            scratch(2, extent_a, wide_b, lanes),
            scratch(2, extent_a, wide_b, lanes),
        ],
        compiler_params=pltpu.CompilerParams(vmem_limit_bytes=VMEM_LIMIT),
        cost_estimate=pl.CostEstimate(
            flops=100 * points, bytes_accessed=8 * points, transcendentals=2 * points
        ),
    )(mine, other, jnp.asarray(third_matrices(lanes)))


def on_device(orbitals, occupations):
    devices, domains = lax.axis_size("band"), lax.axis_size("dom")
    bands, layers, columns, lanes = orbitals.shape
    rows, half, planes = layers // devices, columns // 2, devices // 4
    place = lax.axis_index("band")
    core, side = lax.rem(place, 2), lax.rem(lax.div(place, 2), 2)
    scale = 1.0 / (bands * devices)
    swap_cores = [(i, i ^ 1) for i in range(devices)]

    send, keep = partial_densities(orbitals, occupations, scale)
    other = lax.ppermute(send, "band", swap_cores)
    total, *sends = combine(keep(), other, planes)
    received = [None] * planes
    for step in sorted(range(1, planes), key=lambda step: abs(2 * step - planes)):
        received[step] = lax.ppermute(
            sends[step - 1], "band", [(i, (i + 4 * step) % devices) for i in range(devices)]
        )
    for value in received[1:]:
        total = total + value

    def to(turn, move):
        pairs = []
        for i in range(devices):
            for j in range(domains):
                there = (j + (1 if i % 2 else -1)) % domains if move else j
                pairs.append((i * domains + j, (i ^ turn) * domains + there))
        return pairs

    both = ("band", "dom")
    window = 2 * rows + BEFORE + AFTER
    mine = lax.dynamic_slice_in_dim(total, 2 * rows * side, window, 0)
    theirs = lax.dynamic_slice_in_dim(total, 2 * rows * (1 - side), window, 0)
    mine, theirs = lax.optimization_barrier((mine, theirs))
    own = mine + lax.ppermute(theirs, both, to(2, False))
    beside = lax.ppermute(mine, both, to(0, True)) + lax.ppermute(theirs, both, to(2, True))
    blocks = jnp.stack([own, beside])
    window = rows + BEFORE + AFTER
    mine = lax.dynamic_slice_in_dim(blocks, rows * core, window, 1)
    theirs = lax.dynamic_slice_in_dim(blocks, rows * (1 - core), window, 1)
    return tail(mine, lax.ppermute(theirs, "band", swap_cores), rows)


def solution(mesh):
    return jax.shard_map(
        on_device,
        mesh=mesh,
        in_specs=(P("band", None, "dom", None), P("band")),
        out_specs=P("band", "dom", None),
        check_vma=False,
    )
```
